128 devices in a mesh: tm: 32 (over y, x, core), gz: 4 (over z).
Axes of the slice: x: 4, y: 4, z: 4, core: 2. Of those that a mesh axis runs over, the one named last changes fastest.
Arguments:
- state_rhs: float32 [128, 128, 2048], P('tm', 'gz'), may hold values from -6 to 6
- adjoint_rhs: float32 [128, 128, 2048], P('tm', 'gz'), may hold values from -6 to 6
- diffusivity: float32 [128, 2048], P('gz'), may hold values from 0.02 to 2
- velocity: float32 [3, 128, 2048], P(None, 'gz'), may hold values from -4 to 4
Outputs:
- state_out: float32 [128, 128, 2048], P('tm', 'gz')
- adjoint_out: float32 [128, 128, 2048], P('tm', 'gz')
The draws below stay inside these ranges and needn't reach their ends.
All inputs are finite; a program needn't handle non-finite values.
Results may differ from the reference program's by a relative error of at most 0.0003.
Values sent between devices are 32-bit elements; how exact they have to be, the bound alone decides.
A program may use at most 128 MiB of HBM per device.

```python
import math
import jax
import jax.numpy as jnp
from jax import lax

NY = 64
NXY = 2048
NZ = 128
NT = 128


def block_levels(key, extent, shards, least, high):
    level, own = 1.0, jax.random.fold_in(key, 6)
    for position, blocks in shards:
        heights = jnp.exp(jax.random.uniform(jax.random.fold_in(own, position), (blocks,), jnp.float32, least / len(shards), high / len(shards)))
        level = level * jnp.repeat(heights, extent[position] // blocks).reshape([-1 if axis == position else 1 for axis in range(len(extent))])
    return level


def noise(key, extent, scale, bound, cuts=(), kind=jnp.bfloat16):
    level = block_levels(key, extent, cuts, -0.22, 0.18) if cuts else 1.0
    drawn = jax.random.normal(key, extent, jnp.float32) * scale * level
    return jnp.minimum(jnp.maximum(drawn, -bound), bound).astype(kind)


def setup_inputs(seed: int = 0) -> dict:
    key_of = jax.random.split(jax.random.key(seed), 5)
    return {
        "state_rhs": noise(key_of[0], (NT, NZ, NXY), 1.0, 6.0, ((0, 32), (1, 4)), jnp.float32),
        "adjoint_rhs": noise(key_of[1], (NT, NZ, NXY), 1.0, 6.0, ((0, 32), (1, 4)), jnp.float32),
        "diffusivity": jnp.clip(jnp.exp(math.log(2.0) - 4.6051702 * jax.random.uniform(key_of[2], (NZ, NXY), jnp.float32) ** block_levels(key_of[2], (NZ, NXY), ((0, 4),), -0.2, 0.2)), 0.02, 2.0),
        "velocity": noise(key_of[3], (3, NZ, NXY), 0.8, 4.0, ((1, 4),), jnp.float32),
    }


alpha_wrap = 0.1
beta_couple = 0.5
gamma_couple = 0.5


def ahead_flat(field, stride):
    pad_shape = field.shape[:-1] + (stride,)
    return jnp.concatenate([field[..., stride:], jnp.zeros(pad_shape, field.dtype)], axis=-1)


def behind_flat(field, stride):
    pad_shape = field.shape[:-1] + (stride,)
    return jnp.concatenate([jnp.zeros(pad_shape, field.dtype), field[..., :-stride]], axis=-1)


def neighbour_pairs(field, field_pad, width_y):
    column = jnp.arange(field.shape[-1], dtype=jnp.int32) % width_y
    nothing = jnp.zeros((), field.dtype)
    y_ahead = jnp.where(column == width_y - 1, nothing, ahead_flat(field, 1))
    y_behind = jnp.where(column == 0, nothing, behind_flat(field, 1))
    return [(field_pad[..., 2:, :], field_pad[..., :-2, :]),
            (ahead_flat(field, width_y), behind_flat(field, width_y)),
            (y_ahead, y_behind)]


def face_weights(kappa, kappa_pad, width_y):
    pairs = neighbour_pairs(kappa, kappa_pad, width_y)
    weights = []
    diagonal = jnp.zeros_like(kappa)
    for ahead, behind in pairs:
        face_ahead = jnp.where(ahead > 0.0, 0.5 * (kappa + ahead), kappa)
        face_behind = jnp.where(behind > 0.0, 0.5 * (kappa + behind), kappa)
        weights.append((face_ahead, face_behind))
        diagonal = diagonal + face_ahead + face_behind
    return weights, diagonal


def coupling(field, field_pad, weights, velocity, width_y):
    sign = jnp.array([1.0, -1.0, 1.0, -1.0], field.dtype).reshape((4,) + (1,) * (field.ndim - 1))
    pairs = neighbour_pairs(field, field_pad, width_y)
    speeds = [velocity[2], velocity[0], velocity[1]]
    total = jnp.zeros_like(field)
    for index in range(3):
        ahead, behind = pairs[index]
        face_ahead, face_behind = weights[index]
        total = total + face_ahead * ahead + face_behind * behind - sign * (0.5 * speeds[index]) * (ahead - behind)
    return total


def apply_inverse(stacked, lam_real, lam_imag, diagonal):
    shifted = lam_real + diagonal
    determinant = shifted * shifted + lam_imag * lam_imag + beta_couple * gamma_couple
    state_real, adjoint_real, state_imag, adjoint_imag = stacked[0], stacked[1], stacked[2], stacked[3]
    out_state_real = (shifted * state_real + lam_imag * state_imag + beta_couple * adjoint_real) / determinant
    out_state_imag = (shifted * state_imag - lam_imag * state_real + beta_couple * adjoint_imag) / determinant
    out_adjoint_real = (shifted * adjoint_real - lam_imag * adjoint_imag - gamma_couple * state_real) / determinant
    out_adjoint_imag = (shifted * adjoint_imag + lam_imag * adjoint_real - gamma_couple * state_imag) / determinant
    return jnp.stack([out_state_real, out_adjoint_real, out_state_imag, out_adjoint_imag])


def reference(state_rhs, adjoint_rhs, diffusivity, velocity):
    moments = jnp.arange(NT, dtype=jnp.float32)
    damping = jnp.power(jnp.asarray(alpha_wrap, jnp.float32), moments / NT)
    fields = jnp.stack([state_rhs, adjoint_rhs]) * damping[None, :, None, None]
    spectrum = jnp.fft.fft(fields, axis=1)
    spec_real = jnp.moveaxis(jnp.real(spectrum), 1, 0)
    spec_imag = jnp.moveaxis(jnp.imag(spectrum), 1, 0)
    angle = moments * (2.0 * math.pi / NT)
    ratio = alpha_wrap ** (1.0 / NT)
    lam_real = 1.0 - ratio * jnp.cos(angle)
    lam_imag = ratio * jnp.sin(angle)
    kappa_pad = jnp.pad(diffusivity, ((1, 1), (0, 0)))
    weights, diagonal = face_weights(diffusivity, kappa_pad, NY)

    def solve_one(item):
        part_real, part_imag, one_real, one_imag = item
        stacked = jnp.concatenate([part_real, part_imag])
        first = apply_inverse(stacked, one_real, one_imag, diagonal)
        first_pad = jnp.pad(first, ((0, 0), (1, 1), (0, 0)))
        return apply_inverse(stacked + coupling(first, first_pad, weights, velocity, NY), one_real, one_imag, diagonal)

    solved = lax.map(solve_one, (spec_real, spec_imag, lam_real, lam_imag))
    combined = solved[:, :2] + 1j * solved[:, 2:]
    back = jnp.real(jnp.fft.ifft(combined, axis=0))
    undo = jnp.power(jnp.asarray(alpha_wrap, jnp.float32), -moments / NT)
    result = back * undo[:, None, None, None]
    return result[:, 0], result[:, 1]
```

```python
import functools

import jax
import jax.numpy as jnp
from jax import lax
from jax.experimental import pallas as pl
from jax.experimental.pallas import tpu as pltpu
from jax.sharding import PartitionSpec as P

NY = 64
ALPHA = 0.1
HALF = 0.5
LANES = 128
ROWS = 32
PAD = 8
MESH = pl.DeviceIdType.MESH


def kernel(chips, row, slabs, f_hbm, g_hbm, k_hbm, v_hbm, s_hbm, p_hbm, fg, kp, vel, ck, cn, w, out,
           tot, rx, ct, gat, ret, carr, c2, lsem, osem, ksend, krecv, zsend, zrecv, xsend, xrecv):
    tm = lax.axis_index("tm")
    gz = lax.axis_index("gz")
    chip = tm // 2
    core = tm % 2
    steps = f_hbm.shape[0]
    total = steps * 2 * chips
    q = ALPHA ** (1.0 / total)
    q2 = q * q
    other = (2 * chip + 1 - core, gz)
    up = (tm, lax.rem(gz + 1, slabs))
    down = (tm, lax.rem(gz + slabs - 1, slabs))

    def peer(i):
        y = lax.rem(chip // row + i // row, chips // row)
        x = lax.rem(lax.rem(chip, row) + lax.rem(i, row), row)
        return y * row + x

    def device(c):
        return (2 * c + core, gz)

    barrier = pltpu.get_barrier_semaphore()
    for d in (other, up, down):
        pl.semaphore_signal(barrier, inc=1, device_id=d, device_id_type=MESH)

    def greet(i, _):
        pl.semaphore_signal(barrier, inc=1, device_id=device(peer(i)), device_id_type=MESH)

    lax.fori_loop(1, chips, greet, None)

    def loads(n, j):
        lanes = pl.ds(pl.multiple_of(j * LANES, LANES), LANES)
        source, target = (
            (k_hbm.at[:, lanes], kp.at[j, pl.ds(PAD, ROWS), :]),
            (f_hbm.at[:, :, lanes], fg.at[j, pl.ds(0, steps)]),
            (g_hbm.at[:, :, lanes], fg.at[j, pl.ds(steps, steps)]),
            (v_hbm.at[:, :, lanes], vel.at[j]),
        )[n]
        return pltpu.make_async_copy(source, target, lsem.at[n, j])

    def load_some(which):
        def body(j, _):
            for n in which:
                loads(n, j).start()
        lax.fori_loop(0, chips, body, None)

    load_some((0,))
    load_some((1, 2))
    load_some((3,))

    def wait_kappa(j, _):
        loads(0, j).wait()

    lax.fori_loop(0, chips, wait_kappa, None)
    pl.semaphore_wait(barrier, chips - 1 + 3)

    def edge(direction):
        source, target, device_id = ((PAD + ROWS - 1, PAD - 1, up), (PAD, PAD + ROWS, down))[direction]
        return pltpu.make_async_remote_copy(
            src_ref=kp.at[:, pl.ds(source, 1), :], dst_ref=kp.at[:, pl.ds(target, 1), :],
            send_sem=ksend.at[direction], recv_sem=krecv.at[direction],
            device_id=device_id, device_id_type=MESH)

    edge(0).start()
    edge(1).start()
    edge(0).wait()
    edge(1).wait()

    lane = lax.broadcasted_iota(jnp.int32, (ROWS, LANES), 1)
    line = lax.broadcasted_iota(jnp.int32, (ROWS, LANES), 0)
    ycol = lax.rem(lane, NY)
    first_half = lane < NY

    def sides(ref, j, index):
        here = ref[(j,) + index + (pl.ds(PAD, ROWS),)]
        nxt = ref[(jnp.minimum(j + 1, chips - 1),) + index + (pl.ds(PAD, ROWS),)]
        prv = ref[(jnp.maximum(j - 1, 0),) + index + (pl.ds(PAD, ROWS),)]
        return here, [
            (ref[(j,) + index + (pl.ds(PAD + 1, ROWS),)], ref[(j,) + index + (pl.ds(PAD - 1, ROWS),)]),
            (pltpu.roll(jnp.where(first_half, nxt, here), NY, 1),
             pltpu.roll(jnp.where(first_half, here, prv), NY, 1)),
            (pltpu.roll(here, LANES - 1, 1), pltpu.roll(here, 1, 1)),
        ]

    def faces(j):
        here, pairs = sides(kp, j, ())
        inside = [
            (jnp.logical_or(line < ROWS - 1, gz < slabs - 1), jnp.logical_or(line > 0, gz > 0)),
            (jnp.logical_or(first_half, j < chips - 1), jnp.logical_or(jnp.logical_not(first_half), j > 0)),
            (ycol < NY - 1, ycol > 0),
        ]
        result = []
        for pair, ok in zip(pairs, inside):
            result.append([(jnp.where(m, 0.5 * (here + n), here), m) for n, m in zip(pair, ok)])
        return result

    def waves(j):
        return ck[j, 0], ck[j, 1], ck[j, 2], ck[j, 3]

    def totals(k, j, f, g, b1, b2, mf):
        mb = mf * q2
        fwd = b1 * f[0] + b2 * g[0]
        for n in range(1, steps):
            fwd = b1 * f[n] + b2 * g[n] + mf * fwd
        bwd = b1 * g[steps - 1] - b2 * f[steps - 1]
        for n in range(steps - 2, -1, -1):
            bwd = b1 * g[n] - b2 * f[n] + mb * bwd
        tot[k, 0, j] = fwd
        tot[k, 1, j] = bwd
        to_other(k, j).start()

    def to_other(k, j):
        return pltpu.make_async_remote_copy(
            src_ref=tot.at[k, 1 - core, j], dst_ref=rx.at[k, j],
            send_sem=xsend.at[k, 0, j], recv_sem=xrecv.at[k, 0, j],
            device_id=other, device_id_type=MESH)

    def to_owner(k, j):
        return pltpu.make_async_remote_copy(
            src_ref=ct.at[k, j], dst_ref=gat.at[k, chip],
            send_sem=xsend.at[k, 1, j], recv_sem=xrecv.at[k, 1, chip],
            device_id=device(j), device_id_type=MESH)

    def from_source(k, j):
        return pltpu.make_async_remote_copy(
            src_ref=ct.at[k, j], dst_ref=gat.at[k, j],
            send_sem=xsend.at[k, 1, j], recv_sem=xrecv.at[k, 1, j],
            device_id=device(j), device_id_type=MESH)

    def back(k, j):
        return pltpu.make_async_remote_copy(
            src_ref=ret.at[k, j], dst_ref=carr.at[k, core, chip],
            send_sem=xsend.at[k, 2, j], recv_sem=xrecv.at[k, 2, chip],
            device_id=device(j), device_id_type=MESH)

    def from_owner(k, j):
        return pltpu.make_async_remote_copy(
            src_ref=ret.at[k, j], dst_ref=carr.at[k, core, j],
            send_sem=xsend.at[k, 2, j], recv_sem=xrecv.at[k, 2, j],
            device_id=device(j), device_id_type=MESH)

    def to_other_back(k, j):
        return pltpu.make_async_remote_copy(
            src_ref=c2.at[k, j], dst_ref=carr.at[k, core, j],
            send_sem=xsend.at[k, 3, j], recv_sem=xrecv.at[k, 3, j],
            device_id=other, device_id_type=MESH)

    def from_other_back(k, j):
        return pltpu.make_async_remote_copy(
            src_ref=c2.at[k, j], dst_ref=carr.at[k, 1 - core, j],
            send_sem=xsend.at[k, 3, j], recv_sem=xrecv.at[k, 3, j],
            device_id=other, device_id_type=MESH)

    per_step = jnp.where(core == 0, 1.0, q2).astype(jnp.float32)
    wrap = jnp.where(core == 0, ALPHA, 1.0 / ALPHA).astype(jnp.float32)

    def own_power(j):
        m = ck[j, 2] * per_step
        for _ in range(steps.bit_length() - 1):
            m = m * m
        return m

    def gather(k):
        def send(i, _):
            j = peer(i)
            to_other(k, j).wait_recv()
            ct[k, j] = own_power(j) * tot[k, core, j] + rx[k, j]
            to_owner(k, j).start()

        lax.fori_loop(1, chips, send, None)
        to_other(k, chip).wait_recv()
        gat[k, chip] = own_power(chip) * tot[k, core, chip] + rx[k, chip]

    def scan(k):
        def arrive(i, _):
            from_source(k, peer(i)).wait_recv()

        lax.fori_loop(1, chips, arrive, None)
        m = own_power(chip)
        m = m * m

        def place(r):
            return jnp.where(core == 0, r, chips - 1 - r)

        def step(r, carry):
            return m * carry + gat[k, place(r)]

        whole = lax.fori_loop(0, chips, step, jnp.zeros((ROWS, LANES), jnp.float32))
        m_all = m
        for _ in range(chips.bit_length() - 1):
            m_all = m_all * m_all
        carry = wrap * whole / (1.0 - wrap * m_all)

        def spread(r, carry):
            ret[k, place(r)] = carry
            return m * carry + gat[k, place(r)]

        lax.fori_loop(0, chips, spread, carry)

        def send(i, _):
            back(k, peer(i)).start()

        lax.fori_loop(1, chips, send, None)
        carr[k, core, chip] = ret[k, chip]

        def relay(j):
            c2[k, j] = own_power(j) * carr[k, core, j] + tot[k, core, j]
            to_other_back(k, j).start()

        relay(chip)

        def receive(i, _):
            j = peer(i)
            from_owner(k, j).wait_recv()
            relay(j)

        lax.fori_loop(1, chips, receive, None)

    def solve(k, j, store):
        from_other_back(k, j).wait_recv()
        b1, b2, mf, kf = waves(j)
        mb, kb = mf * q2, kf * q2
        f = [fg[j, n] for n in range(steps)]
        g = [fg[j, steps + n] for n in range(steps)]
        fwd = [carr[k, 0, j]]
        for n in range(steps):
            fwd.append(b1 * f[n] + b2 * g[n] + mf * fwd[-1])
        bwd = [carr[k, 1, j]]
        for n in range(steps - 1, -1, -1):
            bwd.append(b1 * g[n] - b2 * f[n] + mb * bwd[-1])
        bwd = bwd[::-1]
        for n in range(steps):
            store(n, fwd[n + 1] + kb * bwd[n + 1])
            store(steps + n, bwd[n] - kf * fwd[n])

    def begin(i, _):
        j = peer(i)
        a = sum(face for pair in faces(j) for face, _ in pair)
        c = 1.0 + a
        cq = c * q
        m = (c * c + (q2 + HALF * HALF)) / cq
        less = ((c - q) * (c - q) + HALF * HALF) / cq
        rho = 2.0 / (m + jnp.sqrt(less * (m + 2.0)))
        beta = c - q * rho
        scale = rho / (cq * (1.0 - rho * rho))
        b1, b2, mf, kf = scale * beta, HALF * scale, rho * (1.0 / q), rho * (HALF / q) / beta
        ck[j, 0] = b1
        ck[j, 1] = b2
        ck[j, 2] = mf
        ck[j, 3] = kf
        loads(1, j).wait()
        loads(2, j).wait()
        totals(0, j, [fg[j, n] for n in range(steps)], [fg[j, steps + n] for n in range(steps)], b1, b2, mf)

    lax.fori_loop(1, chips + 1, lambda i, _: begin(lax.rem(i, chips), _), None)
    gather(0)

    def couple(j, _):
        loads(3, j).wait()
        sets = faces(j)
        for d, component in enumerate((2, 0, 1)):
            half = 0.5 * vel[j, component]
            (ahead, ok_ahead), (behind, ok_behind) = sets[d]
            for n, value, ok in ((0, ahead - half, ok_ahead), (1, behind + half, ok_behind),
                                 (6, ahead + half, ok_ahead), (7, behind - half, ok_behind)):
                cn[j, 2 * d + n] = jnp.where(ok, value, 0.0)

    lax.fori_loop(0, chips, couple, None)
    scan(0)

    def layer(direction, j):
        source, target, device_id = ((PAD + ROWS - 1, PAD - 1, up), (PAD, PAD + ROWS, down))[direction]
        return pltpu.make_async_remote_copy(
            src_ref=w.at[j, :, pl.ds(source, 1), :], dst_ref=w.at[j, :, pl.ds(target, 1), :],
            send_sem=zsend.at[direction, j], recv_sem=zrecv.at[direction, j],
            device_id=device_id, device_id_type=MESH)

    def first(i, _):
        j = peer(i)

        def store(n, value):
            w[j, n, pl.ds(PAD, ROWS)] = value

        solve(0, j, store)
        layer(0, j).start()
        layer(1, j).start()

    lax.fori_loop(0, chips, first, None)

    def couple_in(i, _):
        j = peer(lax.rem(i, chips))
        layer(0, j).wait_recv()
        layer(1, j).wait_recv()
        fields = []
        for n in range(2 * steps):
            _, pairs = sides(w, j, (n,))
            value = fg[j, n]
            base = 0 if n < steps else 6
            for d in range(3):
                value = value + cn[j, base + 2 * d] * pairs[d][0] + cn[j, base + 2 * d + 1] * pairs[d][1]
            fg[j, n] = value
            fields.append(value)
        b1, b2, mf, _ = waves(j)
        totals(1, j, fields[:steps], fields[steps:], b1, b2, mf)

    lax.fori_loop(1, chips + 1, couple_in, None)
    gather(1)
    scan(1)

    def stores(j):
        lanes = pl.ds(pl.multiple_of(j * LANES, LANES), LANES)
        return [
            pltpu.make_async_copy(out.at[j, pl.ds(0, steps)], s_hbm.at[:, :, lanes], osem.at[0, j]),
            pltpu.make_async_copy(out.at[j, pl.ds(steps, steps)], p_hbm.at[:, :, lanes], osem.at[1, j]),
        ]

    def last(i, _):
        j = peer(i)

        def store(n, value):
            out[j, n] = value

        solve(1, j, store)
        for copy in stores(j):
            copy.start()

    lax.fori_loop(0, chips, last, None)

    def drain(j, _):
        for copy in stores(j):
            copy.wait()
        for k in range(2):
            to_other(k, j).wait_send()
            to_other_back(k, j).wait_send()
        for direction in range(2):
            layer(direction, j).wait_send()

    lax.fori_loop(0, chips, drain, None)

    def drain_peers(i, _):
        for k in range(2):
            to_owner(k, peer(i)).wait_send()
            back(k, peer(i)).wait_send()

    lax.fori_loop(1, chips, drain_peers, None)


def solution(mesh):
    chips = mesh.shape["tm"] // 2
    slabs = mesh.shape["gz"]
    row = 4 if chips % 4 == 0 and chips > 4 else 2

    def body(state_rhs, adjoint_rhs, diffusivity, velocity):
        steps = state_rhs.shape[0]
        chunk = (ROWS, LANES)
        f32 = jnp.float32
        wide = (ROWS + 2 * PAD, LANES)
        hbm = pl.BlockSpec(memory_space=pl.ANY)
        dma = pltpu.SemaphoreType.DMA
        return pl.pallas_call(
            functools.partial(kernel, chips, row, slabs),
            out_shape=[jax.ShapeDtypeStruct(state_rhs.shape, f32)] * 2,
            in_specs=[hbm] * 4,
            out_specs=[hbm] * 2,
            scratch_shapes=[
                pltpu.VMEM((chips, 2 * steps) + chunk, f32),
                pltpu.VMEM((chips,) + wide, f32),
                pltpu.VMEM((chips, 3) + chunk, f32),
                pltpu.VMEM((chips, 4) + chunk, f32),
                pltpu.VMEM((chips, 12) + chunk, f32),
                pltpu.VMEM((chips, 2 * steps) + wide, f32),
                pltpu.VMEM((chips, 2 * steps) + chunk, f32),
                pltpu.VMEM((2, 2, chips) + chunk, f32),
                pltpu.VMEM((2, chips) + chunk, f32),
                pltpu.VMEM((2, chips) + chunk, f32),
                pltpu.VMEM((2, chips) + chunk, f32),
                pltpu.VMEM((2, chips) + chunk, f32),
                pltpu.VMEM((2, 2, chips) + chunk, f32),
                pltpu.VMEM((2, chips) + chunk, f32),
                dma((4, chips)),
                dma((2, chips)),
                dma((2,)),
                dma((2,)),
                dma((2, chips)),
                dma((2, chips)),
                dma((2, 4, chips)),
                dma((2, 4, chips)),
            ],
            compiler_params=pltpu.CompilerParams(
                collective_id=0, has_side_effects=True, vmem_limit_bytes=32 * 1024 * 1024),
        )(state_rhs, adjoint_rhs, diffusivity, velocity)

    placed = (P("tm", "gz", None), P("tm", "gz", None), P("gz", None), P(None, "gz", None))
    return jax.shard_map(
        body,
        mesh=mesh,
        in_specs=placed,
        out_specs=(P("tm", "gz", None), P("tm", "gz", None)),
        check_vma=False,
    )
```
